128 devices in a mesh: layer: 4 (over z), row: 32 (over y, x, core).
Axes of the slice: x: 4, y: 4, z: 4, core: 2. Of those that a mesh axis runs over, the one named last changes fastest.
Arguments:
- rhs_sub: float32 [4, 3, 4096, 256], P('layer', None, 'row'), may hold values from -6 to 6
- rhs_root: float32 [2048, 256], P('row'), may hold values from -6 to 6
- lower_inv: float32 [4, 3, 4096, 4096], P('layer', None, 'row'), may hold values from -0.09375 to 0.09375
- upper_inv: float32 [4, 3, 4096, 4096], P('layer', None, 'row'), may hold values from -0.09375 to 0.09375
- coupling_low: float32 [4, 3, 2048, 4096], P('layer', None, None, 'row'), may hold values from -0.0390625 to 0.0390625
- coupling_up: float32 [4, 3, 4096, 2048], P('layer', None, 'row'), may hold values from -0.1875 to 0.1875
- tile_mask: int32 [4, 3, 16, 32], P('layer', None, None, 'row'), may hold values 0 or 1
- root_inv: float32 [2048, 2048], P('row'), may hold values from -0.125 to 0.125
Outputs:
- sol_sub: float32 [4, 3, 4096, 256], P('layer', None, 'row')
- sol_root: float32 [2048, 256], P('row')
The draws below stay inside these ranges and needn't reach their ends.
All inputs are finite; a program needn't handle non-finite values. No bound on the sum of `tile_mask` on one device may be relied on, other than what follows from the above.
Results may differ from the reference program's by a relative error of at most 0.0001.
Values sent between devices are 32-bit elements; how exact they have to be, the bound alone decides.
No kernel may reach another device: no remote copies, remote signals or barrier semaphores. Data moves between devices by JAX's collectives and lax.ppermute only.
A program may use at most 128 MiB of HBM per device.

```python
import jax
import jax.numpy as jnp
from jax import lax

S = 4096
NA = 2048
TILE = 128
NSUP = 3
NRHS = 256
LAYERS = 4


def set_ends(result, own_key, least, high):
    extent = result.shape
    index_at = [jax.random.randint(jax.random.fold_in(own_key, axis), (), 0, extent[axis]) for axis in range(len(extent))]
    result = result.at[tuple(index_at)].set(least)
    longest = extent.index(max(extent))
    index_at[longest] = (index_at[longest] + 1) % extent[longest]
    return result.at[tuple(index_at)].set(high)


def shard_levels(key, extent, cuts, low, top_value):
    loudness = 1.0
    for axis_at, blocks in cuts:
        heights = jax.random.uniform(jax.random.fold_in(jax.random.fold_in(key, 6), axis_at), (blocks,), jnp.float32, low / len(cuts), top_value / len(cuts))
        loudness = loudness * jnp.repeat(jnp.exp(heights), extent[axis_at] // blocks).reshape((-1,) + (1,) * (len(extent) - 1 - axis_at))
    return loudness


def scatter_about(own_key, extent, spread, bound, cuts=(), held_as=jnp.bfloat16):
    values = spread * jax.random.normal(own_key, extent, jnp.float32)
    if cuts:
        values = values * shard_levels(own_key, extent, cuts, -0.22, 0.18)
    return jnp.clip(values, -bound, bound).astype(held_as)


def setup_inputs(seed: int = 0) -> dict:
    streams_of = jax.random.split(jax.random.key(seed), 9)
    return {
        "rhs_sub": scatter_about(streams_of[0], (LAYERS, NSUP, S, NRHS), 1.0, 6.0, ((0, 4), (2, 32)), jnp.float32),
        "rhs_root": scatter_about(streams_of[1], (NA, NRHS), 1.0, 6.0, ((0, 32),), jnp.float32),
        "lower_inv": scatter_about(streams_of[2], (LAYERS, NSUP, S, S), S ** -0.5, 0.09375, ((0, 4), (2, 32)), jnp.float32),
        "upper_inv": scatter_about(streams_of[3], (LAYERS, NSUP, S, S), S ** -0.5, 0.09375, ((0, 4), (2, 32)), jnp.float32),
        "coupling_low": scatter_about(streams_of[4], (LAYERS, NSUP, NA, S), (S * NSUP * LAYERS // 2) ** -0.5, 0.0390625, ((0, 4), (3, 32)), jnp.float32),
        "coupling_up": scatter_about(streams_of[5], (LAYERS, NSUP, S, NA), (NA // 2) ** -0.5, 0.1875, ((0, 4), (2, 32)), jnp.float32),
        "tile_mask": set_ends((jax.random.randint(streams_of[6], (LAYERS, NSUP, NA // TILE, S // TILE), 0, 2) < 1).astype(jnp.int32), jax.random.fold_in(streams_of[6], 1), 0, 1),
        "root_inv": scatter_about(streams_of[7], (NA, NA), NA ** -0.5, 0.125, ((0, 32),), jnp.float32),
    }


def masked_tiles(coupling, pattern, tile, flipped):
    blocks, height, breadth = coupling.shape
    shaped = coupling.reshape(blocks, height // tile, tile, breadth // tile, tile)
    if flipped:
        pattern = jnp.transpose(pattern, (0, 2, 1))
    weights = pattern.astype(jnp.float32)[:, :, None, :, None]
    return (shaped * weights).reshape(blocks, height, breadth)


def reference(rhs_sub, rhs_root, lower_inv, upper_inv, coupling_low, coupling_up, tile_mask, root_inv):
    highest = lax.Precision.HIGHEST
    interims = []
    total = jnp.zeros(rhs_root.shape, jnp.float32)
    for layer in range(LAYERS):
        row_list = []
        for block in range(NSUP):
            interim = jnp.dot(lower_inv[layer, block], rhs_sub[layer, block], precision=highest, preferred_element_type=jnp.float32)
            weights = masked_tiles(coupling_low[layer, block][None], tile_mask[layer, block][None], TILE, False)[0]
            total = total + jnp.dot(weights, interim, precision=highest, preferred_element_type=jnp.float32)
            row_list.append(interim)
        interims.append(row_list)
    reduced = rhs_root - total
    sol_root = jnp.dot(root_inv, reduced, precision=highest, preferred_element_type=jnp.float32)
    layer_list = []
    for layer in range(LAYERS):
        row_list = []
        for block in range(NSUP):
            weights = masked_tiles(coupling_up[layer, block][None], tile_mask[layer, block][None], TILE, True)[0]
            residue = interims[layer][block] - jnp.dot(weights, sol_root, precision=highest, preferred_element_type=jnp.float32)
            row_list.append(jnp.dot(upper_inv[layer, block], residue, precision=highest, preferred_element_type=jnp.float32))
        layer_list.append(jnp.stack(row_list))
    return jnp.stack(layer_list), sol_root
```

```python
import jax
import jax.numpy as jnp
from jax import lax
from jax.experimental import pallas as pl
from jax.experimental.pallas import tpu as pltpu
from jax.sharding import PartitionSpec as P


TILE = 128
K = 3
CH = 16
F32 = jnp.float32
BF16 = jnp.bfloat16


def row_id(y, x, c):
    return (y % 4) * 8 + (x % 4) * 2 + c % 2


def shift(array, dy, dx, dc=0):
    pairs = [
        (row_id(y, x, c), row_id(y + dy, x + dx, c + dc))
        for y in range(4)
        for x in range(4)
        for c in range(2)
    ]
    return lax.ppermute(array, "row", pairs)


SAME_CORE = [[2 * i + c for i in range(CH)] for c in range(2)]
SAME_CORE_ALL = [[l * 32 + 2 * i + c for l in range(4) for i in range(CH)] for c in range(2)]


def gather_plane(block):
    h = 128
    r, l, u, d = shift(block, 0, 1), shift(block, 0, -1), shift(block, 1, 0), shift(block, -1, 0)
    lo = lambda a: a[:, :h]
    hi = lambda a: a[:, h:]
    r2 = shift(jnp.stack([lo(r), lo(u), lo(d)]), 0, 1)
    l2 = shift(jnp.stack([hi(l), lo(u), lo(d)]), 0, -1)
    u2 = shift(jnp.stack([lo(u), hi(r), hi(l)]), 1, 0)
    d2 = shift(jnp.stack([hi(d), hi(r), hi(l)]), -1, 0)
    xx = jnp.concatenate([r2[0], l2[0]], axis=1)
    yy = jnp.concatenate([u2[0], d2[0]], axis=1)
    r3, l3, u3, d3 = shift(yy, 0, 1), shift(yy, 0, -1), shift(xx, 1, 0), shift(xx, -1, 0)
    q = lambda a, n: a[:, 64 * n : 64 * n + 64]
    r4, l4, u4, d4 = (
        shift(q(r3, 0), 0, 1),
        shift(q(l3, 1), 0, -1),
        shift(q(u3, 2), 1, 0),
        shift(q(d3, 3), -1, 0),
    )
    return [block, r, l, u, d, r2, l2, u2, d2, r3, l3, u3, d3, r4, l4, u4, d4]


PLACES = [
    [(None, 0, 0, 0, 256)],
    [(None, 0, -1, 0, 256)],
    [(None, 0, 1, 0, 256)],
    [(None, -1, 0, 0, 256)],
    [(None, 1, 0, 0, 256)],
    [(0, 0, 2, 0, 128), (1, -1, -1, 0, 128), (2, 1, -1, 0, 128)],
    [(0, 0, 2, 128, 128), (1, -1, 1, 0, 128), (2, 1, 1, 0, 128)],
    [(0, 2, 0, 0, 128), (1, -1, -1, 128, 128), (2, -1, 1, 128, 128)],
    [(0, 2, 0, 128, 128), (1, 1, -1, 128, 128), (2, 1, 1, 128, 128)],
    [(None, 2, -1, 0, 256)],
    [(None, 2, 1, 0, 256)],
    [(None, -1, 2, 0, 256)],
    [(None, 1, 2, 0, 256)],
    [(None, 2, 2, 0, 64)],
    [(None, 2, 2, 64, 64)],
    [(None, 2, 2, 128, 64)],
    [(None, 2, 2, 192, 64)],
]
NP = len(PLACES)


def halves(value):
    top = value.astype(BF16)
    return top, (value - top.astype(F32)).astype(BF16)


def dot(a, b, contract):
    return lax.dot_general(a, b, (contract, ((), ())), preferred_element_type=F32)


def fill_weights(pos, pieces, w_ref):
    y, x = pos[0], pos[1]
    for piece, places in zip(pieces, PLACES):
        for lead, dy, dx, first, rows in places:
            chip = lax.rem(y + (dy + 4), 4) * 4 + lax.rem(x + (dx + 4), 4)
            start = pl.multiple_of(chip * 256 + first, 64)
            for k in range(K):
                value = piece[k] if lead is None else piece[lead, k]
                top, low = halves(value)
                w_ref[k, pl.ds(start, rows), 0:128] = top
                w_ref[k, pl.ds(start, rows), 128:256] = low


def times_weights(matrix, w, contract=((1,), (0,))):
    top, low = halves(matrix)
    wide = dot(top, w, contract) + dot(low, w, contract)
    return wide[:, :128] + wide[:, 128:]


def lower_kernel(pos, *refs):
    pieces = refs[:NP]
    own, part, low_own, low_part, interim, out, own_v, part_v, lo_v, lp_v, w_ref, sems = refs[NP:]
    copies = [
        pltpu.make_async_copy(own, own_v, sems.at[0]),
        pltpu.make_async_copy(part, part_v, sems.at[1]),
        pltpu.make_async_copy(low_own, lo_v, sems.at[2]),
        pltpu.make_async_copy(low_part, lp_v, sems.at[3]),
    ]
    for copy in copies:
        copy.start()
    fill_weights(pos, pieces, w_ref)
    core = pos[2]
    here = pl.multiple_of(core * 128, 128)
    there = pl.multiple_of((1 - core) * 128, 128)
    copies[0].wait()
    copies[1].wait()
    for k in range(K):
        interim[k, pl.ds(here, 128), :] = times_weights(own_v[k], w_ref[k])
        interim[k, pl.ds(there, 128), :] = times_weights(part_v[k], w_ref[k])
    copies[2].wait()
    copies[3].wait()
    ws = []
    for k in range(K):
        for start in (here, there):
            top, low = halves(interim[k, pl.ds(start, 128), :])
            ws.append(jnp.concatenate([top, low], axis=1))
    for i in range(CH):
        rows = pl.ds(i * 128, 128)
        total = jnp.zeros((128, 128), F32)
        for k in range(K):
            total += times_weights(lo_v[k, rows, :], ws[2 * k])
            total += times_weights(lp_v[k, rows, :], ws[2 * k + 1])
        flat = total.T
        for z in range(4):
            out[z, i] = flat[z * 32 : z * 32 + 32]


def upper_kernel(pos, *refs):
    pieces = refs[:NP]
    own, part, out_own, out_part, own_v, part_v, w_ref, sems = refs[NP:]
    copies = [
        pltpu.make_async_copy(own, own_v, sems.at[0]),
        pltpu.make_async_copy(part, part_v, sems.at[1]),
    ]
    for copy in copies:
        copy.start()
    fill_weights(pos, pieces, w_ref)
    copies[0].wait()
    copies[1].wait()
    for k in range(K):
        out_own[k] = times_weights(own_v[k], w_ref[k])
        out_part[k] = times_weights(part_v[k], w_ref[k])


def couple_kernel(pos, root, interim, own, part, residue, own_v, part_v, w_ref, sems):
    copies = [
        pltpu.make_async_copy(own, own_v, sems.at[0]),
        pltpu.make_async_copy(part, part_v, sems.at[1]),
    ]
    for copy in copies:
        copy.start()
    for i in range(CH):
        top, low = halves(jnp.concatenate([root[z, i] for z in range(4)], axis=0))
        w_ref[0:128, i * 128 : i * 128 + 128] = top
        w_ref[128:256, i * 128 : i * 128 + 128] = low
    core = pos[2]
    here = pl.ds(pl.multiple_of(core * 128, 128), 128)
    there = pl.ds(pl.multiple_of((1 - core) * 128, 128), 128)
    copies[0].wait()
    copies[1].wait()
    last = ((1,), (1,))
    for k in range(K):
        residue[k, here, :] = interim[k, here, :] - times_weights(own_v[k], w_ref[...], last)
        residue[k, there, :] = interim[k, there, :] - times_weights(part_v[k], w_ref[...], last)


VMEM = pl.BlockSpec(memory_space=pltpu.VMEM)
ANY = pl.BlockSpec(memory_space=pl.ANY)
SMEM = pl.BlockSpec(memory_space=pltpu.SMEM)
sds = lambda *shape: jax.ShapeDtypeStruct(shape, F32)
LIMIT = pltpu.CompilerParams(vmem_limit_bytes=56 * 1024 * 1024)


def run_lower(pos, pieces, own, part, low_own, low_part):
    return pl.pallas_call(
        lower_kernel,
        out_shape=(sds(K, 256, 128), sds(4, CH, 32, 128)),
        in_specs=[SMEM] + [VMEM] * NP + [ANY] * 4,
        out_specs=(VMEM, VMEM),
        scratch_shapes=[
            pltpu.VMEM((K, 128, 4096), F32),
            pltpu.VMEM((K, 128, 4096), F32),
            pltpu.VMEM((K, 2048, 128), F32),
            pltpu.VMEM((K, 2048, 128), F32),
            pltpu.VMEM((K, 4096, 256), BF16),
            pltpu.SemaphoreType.DMA((4,)),
        ],
        compiler_params=LIMIT,
    )(pos, *pieces, own, part, low_own, low_part)


def run_upper(pos, pieces, own, part):
    return pl.pallas_call(
        upper_kernel,
        out_shape=(sds(K, 128, 128), sds(K, 128, 128)),
        in_specs=[SMEM] + [VMEM] * NP + [ANY] * 2,
        out_specs=(VMEM, VMEM),
        scratch_shapes=[
            pltpu.VMEM((K, 128, 4096), F32),
            pltpu.VMEM((K, 128, 4096), F32),
            pltpu.VMEM((K, 4096, 256), BF16),
            pltpu.SemaphoreType.DMA((2,)),
        ],
        compiler_params=LIMIT,
    )(pos, *pieces, own, part)


def run_couple(pos, root, interim, own, part):
    return pl.pallas_call(
        couple_kernel,
        out_shape=sds(K, 256, 128),
        in_specs=[SMEM, VMEM, VMEM, ANY, ANY],
        out_specs=VMEM,
        scratch_shapes=[
            pltpu.VMEM((K, 128, 2048), F32),
            pltpu.VMEM((K, 128, 2048), F32),
            pltpu.VMEM((256, 2048), BF16),
            pltpu.SemaphoreType.DMA((2,)),
        ],
        compiler_params=LIMIT,
    )(pos, root, interim, own, part)


def body(rhs_sub, rhs_root, lower_inv, upper_inv, coupling_low, coupling_up, tile_mask, root_inv):
    me = lax.axis_index("row")
    layer = lax.axis_index("layer")
    core = me % 2
    pos = jnp.stack([me // 8, me // 2 % 4, core]).astype(jnp.int32)
    first = core == 0
    swap = lambda a: shift(a, 0, 0, 1)

    def to_columns(a):
        left, right = a[..., :128], a[..., 128:]
        mine, other = jnp.where(first, left, right), jnp.where(first, right, left)
        got = swap(other)
        return jnp.where(
            first, jnp.concatenate([mine, got], axis=-2), jnp.concatenate([got, mine], axis=-2)
        )

    def to_rows(mine, other):
        got = swap(other)
        return jnp.where(
            first, jnp.concatenate([mine, got], axis=-1), jnp.concatenate([got, mine], axis=-1)
        )

    mask = tile_mask[0, :, :, 0].astype(F32)
    block = to_columns(rhs_sub[0])
    pieces = gather_plane(block)
    lower_own = lower_inv[0]
    lower_part = swap(lower_own)
    low_own = (coupling_low[0].reshape(K, CH, TILE, TILE) * mask[:, :, None, None]).reshape(
        K, CH * TILE, TILE
    )
    low_part = swap(low_own)
    up_own = (coupling_up[0].reshape(K, TILE, CH, TILE) * mask[:, None, :, None]).reshape(
        K, TILE, CH * TILE
    )
    up_part = swap(up_own)
    upper_own = upper_inv[0]
    upper_part = swap(upper_own)
    root_other = swap(root_inv)
    root_rows = jnp.where(
        first,
        jnp.concatenate([root_inv, root_other], axis=0),
        jnp.concatenate([root_other, root_inv], axis=0),
    )
    right = lax.dynamic_slice_in_dim(to_columns(rhs_root).T, layer * 32, 32, 0)

    interim, parts = run_lower(pos, pieces, lower_own, lower_part, low_own, low_part)
    moved = lax.all_to_all(
        parts.reshape(64, 32, 128), ("layer", "row"), 0, 0, tiled=True,
        axis_index_groups=SAME_CORE_ALL,
    )
    reduced = right - jnp.sum(moved, axis=0)
    everywhere = lax.all_to_all(
        jnp.broadcast_to(reduced[None], (CH, 32, 128)), "row", 0, 0, tiled=True,
        axis_index_groups=SAME_CORE,
    )
    solved = jnp.einsum(
        "icr,oir->co", everywhere, root_rows.reshape(128, CH, 128), precision=lax.Precision.HIGHEST
    )
    root = lax.all_to_all(
        jnp.broadcast_to(solved[None], (64, 32, 128)), ("layer", "row"), 0, 0, tiled=True,
        axis_index_groups=SAME_CORE_ALL,
    ).reshape(4, CH, 32, 128)
    residue = run_couple(pos, root, interim, up_own, up_part)
    out_own, out_part = run_upper(pos, gather_plane(residue), upper_own, upper_part)
    sol_sub = to_rows(out_own, out_part)

    chip = me // 2
    mine = lax.dynamic_index_in_dim(root, chip, 1, keepdims=False).reshape(128, 128).T
    own_rows = lax.dynamic_slice_in_dim(mine, core * 64, 64, 0)
    other_rows = lax.dynamic_slice_in_dim(mine, (1 - core) * 64, 64, 0)
    return sol_sub[None], to_rows(own_rows, other_rows)


def solution(mesh):
    return jax.shard_map(
        body,
        mesh=mesh,
        in_specs=(
            P("layer", None, "row", None),
            P("row", None),
            P("layer", None, "row", None),
            P("layer", None, "row", None),
            P("layer", None, None, "row"),
            P("layer", None, "row", None),
            P("layer", None, None, "row"),
            P("row", None),
        ),
        out_specs=(P("layer", None, "row", None), P("row", None)),
        check_vma=False,
    )
```

```python
import functools

import jax
import jax.numpy as jnp
from jax import lax
from jax.experimental import pallas as pl
from jax.experimental.pallas import tpu as pltpu
from jax.sharding import PartitionSpec as P


TILE = 128
K = 3
CH = 16
F32 = jnp.float32
BF16 = jnp.bfloat16


def row_id(y, x, c):
    return (y % 4) * 8 + (x % 4) * 2 + c % 2


def shift(array, da, db):
    pairs = []
    for y in range(4):
        for x in range(4):
            pairs.append((row_id(y, x, 0), row_id(y + db, x + da, 0)))
            pairs.append((row_id(y, x, 1), row_id(y + da, x + db, 1)))
    return lax.ppermute(array, "row", pairs)


def swap(array):
    return lax.ppermute(array, "row", [(i, i ^ 1) for i in range(32)])


SAME_CORE = [[2 * i + c for i in range(CH)] for c in range(2)]
SAME_CORE_ALL = [[l * 32 + 2 * i + c for l in range(4) for i in range(CH)] for c in range(2)]

STAGE_1 = [(0, 0), (-1, 0), (1, 0), (2, 0)]
STAGE_2 = [(0, -1), (-1, -1), (0, 1), (-1, 1), (1, -1), (2, -1), (1, 1), (2, 1)]
STAGE_3 = [(0, 2), (-1, 2), (1, 2), (2, 2)]


def gather_plane(block):
    left, right, far = shift(block, 1, 0), shift(block, -1, 0), shift(block, 2, 0)
    a = jnp.stack([block, left])
    a_up, a_down = shift(a, 0, 1), shift(a, 0, -1)
    b = jnp.stack([right, far])
    b_up, b_down = shift(b, 0, 1), shift(b, 0, -1)
    a_far, b_far = shift(a_up, 0, 1), shift(b_down, 0, -1)
    return [block, left, right, far], [a_up, a_down, b_up, b_down], [a_far, b_far]


def halves(value):
    top = value.astype(BF16)
    return top, (value - top.astype(F32)).astype(BF16)


def stacked(value, axis):
    return jnp.concatenate(halves(value), axis=axis)


def product(rows, w):
    n = rows.shape[0] // 2
    wide = jnp.dot(rows, w, preferred_element_type=F32)
    tall = wide[:n] + wide[n:]
    return tall[:, :128] + tall[:, 128:]


def chip_of(pos, da, db):
    core = pos[2]
    dy, dx = db + core * (da - db), da + core * (db - da)
    return lax.rem(pos[0] + dy + 4, 4) * 4 + lax.rem(pos[1] + dx + 4, 4)


def start_columns(pos, stage, own, part, lv, sems):
    copies = []
    for j, (da, db) in enumerate(stage):
        columns = pl.ds(pl.multiple_of(chip_of(pos, da, db) * 256, 256), 256)
        here = slice(j * 256, j * 256 + 256)
        copies.append(
            pltpu.make_async_copy(own.at[:, :, columns], lv.at[:, 0:128, here], sems.at[2 * j])
        )
        copies.append(
            pltpu.make_async_copy(part.at[:, :, columns], lv.at[:, 128:256, here], sems.at[2 * j + 1])
        )
    for copy in copies:
        copy.start()
    return copies


def fill(pieces, w):
    j = 0
    for piece in pieces:
        for lead in range(piece.shape[0] if len(piece.shape) == 4 else 1):
            for k in range(K):
                value = piece[lead, k] if len(piece.shape) == 4 else piece[k]
                w[k, j * 256 : j * 256 + 256, :] = stacked(value, 1)
            j += 1


def add_kernel(stage, n, has_total, pos, *refs):
    refs = list(refs)
    total = refs.pop(0) if has_total else None
    pieces = refs[:n]
    own, part, out, lv, w, sems = refs[n:]
    copies = start_columns(pos, stage, own, part, lv, sems)
    fill(pieces, w)
    for copy in copies:
        copy.wait()
    for k in range(K):
        value = product(stacked(lv[k], 0), w[k])
        out[k] = value if total is None else total[k] + value


def lower_kernel(stage, n, pos, total, *refs):
    pieces = refs[:n]
    own, part, low, interim, out, lv, w, low_v, sems = refs[n:]
    copies = start_columns(pos, stage, own, part, lv, sems)
    low_copy = pltpu.make_async_copy(low, low_v, sems.at[2 * len(stage)])
    low_copy.start()
    fill(pieces, w)
    for copy in copies:
        copy.wait()
    weights = []
    for k in range(K):
        value = total[k] + product(stacked(lv[k], 0), w[k])
        interim[k] = value
        weights.append(stacked(value, 1))
    low_copy.wait()
    for c in range(4):
        roots = product(low_v[0, c], weights[0])
        for k in range(1, K):
            roots += product(low_v[k, c], weights[k])
        for i in range(4):
            flat = roots[i * 128 : i * 128 + 128].T
            for z in range(4):
                out[z, 4 * c + i] = flat[z * 32 : z * 32 + 32]


def upper_kernel(stage, n, pos, total, *refs):
    pieces = refs[:n]
    own, part, out, out_part, lv, w, sems = refs[n:]
    copies = start_columns(pos, stage, own, part, lv, sems)
    fill(pieces, w)
    for copy in copies:
        copy.wait()
    lanes = pl.ds(pl.multiple_of(pos[2] * 128, 128), 128)
    for k in range(K):
        value = total[k] + product(stacked(lv[k], 0), w[k])
        out[k, :, lanes] = value[:128]
        out_part[k] = value[128:]


def couple_kernel(pos, root, interim, up, residue, w):
    for i in range(CH):
        flat = jnp.concatenate([root[z, i] for z in range(4)], axis=0)
        w[i * 128 : i * 128 + 128, :] = stacked(flat.T, 1)
    here = pl.ds(pl.multiple_of(pos[2] * 128, 128), 128)
    there = pl.ds(pl.multiple_of((1 - pos[2]) * 128, 128), 128)
    for k in range(K):
        value = interim[k] - product(up[k], w[...])
        residue[k, here, :] = value[:128]
        residue[k, there, :] = value[128:]


def low_kernel(mask, own, part, out):
    for i in range(4):
        rows = slice(i * 128, i * 128 + 128)
        value = jnp.concatenate([own[0, rows], part[0, rows]], axis=1) * mask[0, 0, i : i + 1, :]
        top, low = halves(value)
        out[0, 0, rows] = top
        out[0, 0, slice(512 + i * 128, 640 + i * 128)] = low


def up_kernel(mask, own, part, out):
    for n, ref in enumerate((own, part)):
        top, low = halves(ref[0] * mask[0, n : n + 1, :])
        out[0, n * 128 : n * 128 + 128] = top
        out[0, 256 + n * 128 : 384 + n * 128] = low


VMEM = pl.BlockSpec(memory_space=pltpu.VMEM)
ANY = pl.BlockSpec(memory_space=pl.ANY)
SMEM = pl.BlockSpec(memory_space=pltpu.SMEM)


def sds(*shape, dtype=F32):
    return jax.ShapeDtypeStruct(shape, dtype)


def limit(mib):
    return pltpu.CompilerParams(vmem_limit_bytes=mib * 1024 * 1024)


def stage_scratch(n):
    return [pltpu.VMEM((K, 256, n * 256), F32), pltpu.VMEM((K, n * 256, 256), BF16)]


def run_add(pos, stage, total, pieces, own, part):
    first = [] if total is None else [total]
    return pl.pallas_call(
        functools.partial(add_kernel, stage, len(pieces), total is not None),
        out_shape=sds(K, 256, 128),
        in_specs=[SMEM] + [VMEM] * (len(first) + len(pieces)) + [ANY] * 2,
        out_specs=VMEM,
        scratch_shapes=stage_scratch(len(stage)) + [pltpu.SemaphoreType.DMA((2 * len(stage),))],
        compiler_params=limit(40),
    )(pos, *first, *pieces, own, part)


def run_lower(pos, stage, total, pieces, own, part, low):
    return pl.pallas_call(
        functools.partial(lower_kernel, stage, len(pieces)),
        out_shape=(sds(K, 256, 128), sds(4, CH, 32, 128)),
        in_specs=[SMEM] + [VMEM] * (1 + len(pieces)) + [ANY] * 3,
        out_specs=(VMEM, VMEM),
        scratch_shapes=stage_scratch(len(stage))
        + [pltpu.VMEM((K, 4, 1024, 256), BF16), pltpu.SemaphoreType.DMA((2 * len(stage) + 1,))],
        compiler_params=limit(40),
    )(pos, total, *pieces, own, part, low)


def run_upper(pos, stage, total, pieces, own, part):
    return pl.pallas_call(
        functools.partial(upper_kernel, stage, len(pieces)),
        out_shape=(sds(K, 128, 256), sds(K, 128, 128)),
        in_specs=[SMEM] + [VMEM] * (1 + len(pieces)) + [ANY] * 2,
        out_specs=(VMEM, VMEM),
        scratch_shapes=stage_scratch(len(stage)) + [pltpu.SemaphoreType.DMA((2 * len(stage),))],
        compiler_params=limit(40),
    )(pos, total, *pieces, own, part)


def run_couple(pos, root, interim, up):
    return pl.pallas_call(
        couple_kernel,
        out_shape=sds(K, 256, 128),
        in_specs=[SMEM, VMEM, VMEM, VMEM],
        out_specs=VMEM,
        scratch_shapes=[pltpu.VMEM((2048, 256), BF16)],
        compiler_params=limit(40),
    )(pos, root, interim, up)


def run_low(mask, own, part):
    block = pl.BlockSpec((1, 512, 128), lambda k, c: (k, c, 0))
    return pl.pallas_call(
        low_kernel,
        out_shape=sds(K, 4, 1024, 256, dtype=BF16),
        grid=(K, 4),
        in_specs=[pl.BlockSpec((1, 1, 4, 256), lambda k, c: (k, c, 0, 0)), block, block],
        out_specs=pl.BlockSpec((1, 1, 1024, 256), lambda k, c: (k, c, 0, 0)),
        compiler_params=limit(20),
    )(mask, own, part)


def run_up(mask, own, part):
    block = pl.BlockSpec((1, 128, 2048), lambda k: (k, 0, 0))
    return pl.pallas_call(
        up_kernel,
        out_shape=sds(K, 512, 2048, dtype=BF16),
        grid=(K,),
        in_specs=[pl.BlockSpec((1, 2, 2048), lambda k: (k, 0, 0)), block, block],
        out_specs=pl.BlockSpec((1, 512, 2048), lambda k: (k, 0, 0)),
        compiler_params=limit(20),
    )(mask, own, part)


def body(rhs_sub, rhs_root, lower_inv, upper_inv, coupling_low, coupling_up, tile_mask, root_inv):
    me = lax.axis_index("row")
    layer = lax.axis_index("layer")
    core = me % 2
    pos = jnp.stack([me // 8, me // 2 % 4, core]).astype(jnp.int32)
    first = core == 0

    def to_columns(a):
        left, right = a[..., :128], a[..., 128:]
        mine, other = jnp.where(first, left, right), jnp.where(first, right, left)
        got = swap(other)
        return jnp.where(
            first, jnp.concatenate([mine, got], axis=-2), jnp.concatenate([got, mine], axis=-2)
        )

    block = to_columns(rhs_sub[0])
    block, rhs_root, lower_own, low_own, up_own, root_inv, tile_mask = lax.optimization_barrier(
        (block, rhs_root, lower_inv[0], coupling_low[0], coupling_up[0], root_inv, tile_mask)
    )
    one, two, three = gather_plane(block)
    lower_part = swap(lower_own)
    mask_own = tile_mask[0, :, :, 0].astype(F32)
    mask_part = swap(mask_own)
    right = lax.dynamic_slice_in_dim(to_columns(rhs_root).T, layer * 32, 32, 0)
    low_part = swap(low_own)
    up_part = swap(up_own)
    spread = lambda m, n: jnp.broadcast_to(m[..., None], m.shape + (n,))
    low_mask = jnp.concatenate([spread(mask_own, 128), spread(mask_part, 128)], axis=-1)
    low_mask, right = lax.optimization_barrier((low_mask.reshape(K, 4, 4, 256), right))
    low = run_low(low_mask, low_own, low_part)
    up_mask = jnp.stack(
        [spread(mask_own, 128).reshape(K, 2048), spread(mask_part, 128).reshape(K, 2048)], axis=1
    )
    up = run_up(up_mask, up_own, up_part)

    total = run_add(pos, STAGE_1, None, one, lower_own, lower_part)
    total, upper_own = lax.optimization_barrier((total, upper_inv[0]))
    upper_part = swap(upper_own)
    root_other = swap(root_inv)
    root_rows = jnp.where(
        first,
        jnp.concatenate([root_inv, root_other], axis=0),
        jnp.concatenate([root_other, root_inv], axis=0),
    )
    total = run_add(pos, STAGE_2, total, two, lower_own, lower_part)
    interim, parts = run_lower(pos, STAGE_3, total, three, lower_own, lower_part, low)
    moved = lax.all_to_all(
        parts.reshape(64, 32, 128), ("layer", "row"), 0, 0, tiled=True,
        axis_index_groups=SAME_CORE_ALL,
    )
    reduced = right - jnp.sum(moved, axis=0)
    everywhere = lax.all_to_all(
        jnp.broadcast_to(reduced[None], (CH, 32, 128)), "row", 0, 0, tiled=True,
        axis_index_groups=SAME_CORE,
    )
    solved = jnp.einsum(
        "icr,oir->co", everywhere, root_rows.reshape(128, CH, 128), precision=lax.Precision.HIGHEST
    )
    root = lax.all_to_all(
        jnp.broadcast_to(solved[None], (64, 32, 128)), ("layer", "row"), 0, 0, tiled=True,
        axis_index_groups=SAME_CORE_ALL,
    ).reshape(4, CH, 32, 128)
    residue = run_couple(pos, root, interim, up)
    one, two, three = gather_plane(residue)
    total = run_add(pos, STAGE_1, None, one, upper_own, upper_part)
    total = run_add(pos, STAGE_2, total, two, upper_own, upper_part)
    out, out_part = run_upper(pos, STAGE_3, total, three, upper_own, upper_part)
    sol_sub = lax.dynamic_update_slice(out, swap(out_part), (0, 0, (1 - core) * 128))

    chip = me // 2
    mine = lax.dynamic_index_in_dim(root, chip, 1, keepdims=False).reshape(128, 128).T
    own_rows = lax.dynamic_slice_in_dim(mine, core * 64, 64, 0)
    other_rows = swap(lax.dynamic_slice_in_dim(mine, (1 - core) * 64, 64, 0))
    sol_root = jnp.where(
        first,
        jnp.concatenate([own_rows, other_rows], axis=-1),
        jnp.concatenate([other_rows, own_rows], axis=-1),
    )
    return sol_sub[None], sol_root


def solution(mesh):
    return jax.shard_map(
        body,
        mesh=mesh,
        in_specs=(
            P("layer", None, "row", None),
            P("row", None),
            P("layer", None, "row", None),
            P("layer", None, "row", None),
            P("layer", None, None, "row"),
            P("layer", None, "row", None),
            P("layer", None, None, "row"),
            P("row", None),
        ),
        out_specs=(P("layer", None, "row", None), P("row", None)),
        check_vma=False,
    )
```

```python
import functools

import jax
import jax.numpy as jnp
from jax import lax
from jax.experimental import pallas as pl
from jax.experimental.pallas import tpu as pltpu
from jax.sharding import PartitionSpec as P


K = 3
CH = 16
F32 = jnp.float32
BF16 = jnp.bfloat16


def row_id(y, x, c):
    return (y % 4) * 8 + (x % 4) * 2 + c % 2


def shift(array, da, db):
    pairs = []
    for y in range(4):
        for x in range(4):
            pairs.append((row_id(y, x, 0), row_id(y + db, x + da, 0)))
            pairs.append((row_id(y, x, 1), row_id(y + da, x + db, 1)))
    return lax.ppermute(array, "row", pairs)


def swap(array):
    return lax.ppermute(array, "row", [(i, i ^ 1) for i in range(32)])


SAME_CORE = [[2 * i + c for i in range(CH)] for c in range(2)]
SAME_CORE_ALL = [[l * 32 + 2 * i + c for l in range(4) for i in range(CH)] for c in range(2)]

FIRST = [(0, 0), (1, 0), (-1, 0), (2, 0), (0, -1), (0, 1), (1, -1), (1, 1)]
SECOND = [(-1, -1), (-1, 1), (2, -1), (2, 1)]
LATE = [(0, 2), (1, 2), (-1, 2), (2, 2)]


def gather_plane(own):
    move = lambda v, da, db: shift(v, da, db)
    right, left = move(own, -1, 0), move(own, 1, 0)
    far = move(own, 2, 0)
    ups, downs = [], []
    for value in (own, right, left, far):
        ups.append(move(value, 0, 1))
        downs.append(move(value, 0, -1))
    late = [move(downs[0], 0, -1), move(downs[1], 0, -1), move(ups[2], 0, 1), move(downs[3], 0, -1)]
    first = [own, right, left, far, ups[0], downs[0], ups[1], downs[1]]
    return first, [ups[2], downs[2], ups[3], downs[3]], late


def halves(value):
    top = value.astype(BF16)
    return top, (value - top.astype(F32)).astype(BF16)


def stacked(value, axis):
    return jnp.concatenate(halves(value), axis=axis)


def product(rows, w):
    n = rows.shape[0] // 2
    wide = jnp.dot(rows, w, preferred_element_type=F32)
    tall = wide[:n] + wide[n:]
    return tall[:, :128] + tall[:, 128:]


def chip_of(pos, da, db):
    core = pos[2]
    dy, dx = db + core * (da - db), da + core * (db - da)
    return lax.rem(pos[0] + dy + 4, 4) * 4 + lax.rem(pos[1] + dx + 4, 4)


def start_stage(pos, stage, pieces, own, part, lv, pv, sems):
    columns = [
        pl.ds(pl.multiple_of(chip_of(pos, da, db) * 256, 256), 256) for da, db in stage
    ]
    waits = []
    for k in range(K):
        copies = []
        for j, piece in enumerate(pieces):
            copies.append((piece.at[k], pv.at[k, j]))
        for j, column in enumerate(columns):
            here = slice(j * 256, j * 256 + 256)
            copies.append((own.at[k, :, column], lv.at[k, 0:128, here]))
            copies.append((part.at[k, :, column], lv.at[k, 128:256, here]))
        copies = [
            pltpu.make_async_copy(src, dst, sems.at[k, i]) for i, (src, dst) in enumerate(copies)
        ]
        for copy in copies:
            copy.start()
        waits.append(copies)
    return waits


def stage_product(waits, k, lv, pv, w):
    for copy in waits[k]:
        copy.wait()
    for j in range(pv.shape[1]):
        w[k, j * 256 : j * 256 + 256, :] = stacked(pv[k, j], 1)
    return product(stacked(lv[k], 0), w[k])


def add_kernel(stage, has_total, pos, *refs):
    total, refs = (refs[0], refs[1:]) if has_total else (None, refs)
    pieces = refs[: len(stage)]
    own, part, out, lv, pv, w, sems = refs[len(stage) :]
    waits = start_stage(pos, stage, pieces, own, part, lv, pv, sems)
    for k in range(K):
        value = stage_product(waits, k, lv, pv, w)
        out[k] = total[k] + value if has_total else value


def lower_kernel(n, pos, mask_own, mask_part, total, *refs):
    pieces = refs[:n]
    own, part, low_own, low_part, interim, out, lv, pv, w, lo_v, lp_v, sems, low_sems = refs[n:]
    waits = start_stage(pos, LATE, pieces, own, part, lv, pv, sems)
    low_copies = []
    for c in range(4):
        rows = slice(c * 512, c * 512 + 512)
        low_copies.append(
            [
                pltpu.make_async_copy(low_own.at[:, rows], lo_v.at[:, rows], low_sems.at[c, 0]),
                pltpu.make_async_copy(low_part.at[:, rows], lp_v.at[:, rows], low_sems.at[c, 1]),
            ]
        )
        for copy in low_copies[-1]:
            copy.start()
    weights = []
    for k in range(K):
        value = total[k] + stage_product(waits, k, lv, pv, w)
        interim[k] = value
        weights.append(stacked(value, 1))
    for c in range(4):
        for copy in low_copies[c]:
            copy.wait()
        roots = None
        for k in range(K):
            tiles = []
            for i in range(4 * c, 4 * c + 4):
                rows = slice(i * 128, i * 128 + 128)
                tiles.append(
                    jnp.concatenate(
                        [
                            lo_v[k, rows, :] * mask_own[k, i, 0].astype(F32),
                            lp_v[k, rows, :] * mask_part[k, i, 0].astype(F32),
                        ],
                        axis=1,
                    )
                )
            value = product(stacked(jnp.concatenate(tiles, axis=0), 0), weights[k])
            roots = value if roots is None else roots + value
        for i in range(4):
            flat = roots[i * 128 : i * 128 + 128].T
            for z in range(4):
                out[z, 4 * c + i] = flat[z * 32 : z * 32 + 32]


def upper_kernel(n, pos, total, *refs):
    pieces = refs[:n]
    own, part, out, out_part, lv, pv, w, sems = refs[n:]
    waits = start_stage(pos, LATE, pieces, own, part, lv, pv, sems)
    lanes = pl.ds(pl.multiple_of(pos[2] * 128, 128), 128)
    for k in range(K):
        value = total[k] + stage_product(waits, k, lv, pv, w)
        out[k, :, lanes] = value[:128]
        out_part[k] = value[128:]


def couple_kernel(pos, root, interim, up, residue, up_v, w, sems):
    copies = [pltpu.make_async_copy(up.at[k], up_v.at[k], sems.at[k]) for k in range(K)]
    for copy in copies:
        copy.start()
    for i in range(CH):
        flat = jnp.concatenate([root[z, i] for z in range(4)], axis=0)
        w[i * 128 : i * 128 + 128, :] = stacked(flat.T, 1)
    here = pl.ds(pl.multiple_of(pos[2] * 128, 128), 128)
    there = pl.ds(pl.multiple_of((1 - pos[2]) * 128, 128), 128)
    for k in range(K):
        copies[k].wait()
        value = interim[k] - product(up_v[k], w[...])
        residue[k, here, :] = value[:128]
        residue[k, there, :] = value[128:]


def up_kernel(mask_own, mask_part, own, part, out):
    k = pl.program_id(0)
    for n, (mask, ref) in enumerate(((mask_own, own), (mask_part, part))):
        for i in range(CH):
            lanes = slice(i * 128, i * 128 + 128)
            top, low = halves(ref[0, :, lanes] * mask[k, i, 0].astype(F32))
            out[0, n * 128 : n * 128 + 128, lanes] = top
            out[0, 256 + n * 128 : 384 + n * 128, lanes] = low


BIG = 58
VMEM = pl.BlockSpec(memory_space=pltpu.VMEM)
HBM = pl.BlockSpec(memory_space=pltpu.HBM)
SMEM = pl.BlockSpec(memory_space=pltpu.SMEM)


def sds(*shape, dtype=F32):
    return jax.ShapeDtypeStruct(shape, dtype)


def limit(mib):
    return pltpu.CompilerParams(vmem_limit_bytes=mib * 1024 * 1024)


def stage_scratch(stage, pieces):
    n = len(stage)
    return [
        pltpu.VMEM((K, 256, n * 256), F32),
        pltpu.VMEM((K, n, 256, 128), F32),
        pltpu.VMEM((K, n * 256, 256), BF16),
        pltpu.SemaphoreType.DMA((K, 2 * n + len(pieces))),
    ]


def run_add(pos, stage, total, pieces, own, part):
    totals = [] if total is None else [total]
    return pl.pallas_call(
        functools.partial(add_kernel, stage, total is not None),
        out_shape=sds(K, 256, 128),
        in_specs=[SMEM] + [VMEM] * len(totals) + [HBM] * (len(pieces) + 2),
        out_specs=VMEM,
        scratch_shapes=stage_scratch(stage, pieces),
        compiler_params=limit(BIG),
    )(pos, *totals, *pieces, own, part)


def run_lower(pos, mask_own, mask_part, total, pieces, own, part, low_own, low_part):
    scratch = stage_scratch(LATE, pieces)
    return pl.pallas_call(
        functools.partial(lower_kernel, len(pieces)),
        out_shape=(sds(K, 256, 128), sds(4, CH, 32, 128)),
        in_specs=[SMEM] * 3 + [VMEM] + [HBM] * (len(pieces) + 4),
        out_specs=(VMEM, VMEM),
        scratch_shapes=scratch[:3]
        + [
            pltpu.VMEM((K, 2048, 128), F32),
            pltpu.VMEM((K, 2048, 128), F32),
            scratch[3],
            pltpu.SemaphoreType.DMA((4, 2)),
        ],
        compiler_params=limit(BIG),
    )(pos, mask_own, mask_part, total, *pieces, own, part, low_own, low_part)


def run_upper(pos, total, pieces, own, part):
    return pl.pallas_call(
        functools.partial(upper_kernel, len(pieces)),
        out_shape=(sds(K, 128, 256), sds(K, 128, 128)),
        in_specs=[SMEM, VMEM] + [HBM] * (len(pieces) + 2),
        out_specs=(VMEM, VMEM),
        scratch_shapes=stage_scratch(LATE, pieces),
        compiler_params=limit(BIG),
    )(pos, total, *pieces, own, part)


def run_couple(pos, root, interim, up):
    return pl.pallas_call(
        couple_kernel,
        out_shape=sds(K, 256, 128),
        in_specs=[SMEM, VMEM, VMEM, HBM],
        out_specs=VMEM,
        scratch_shapes=[
            pltpu.VMEM((K, 512, 2048), BF16),
            pltpu.VMEM((2048, 256), BF16),
            pltpu.SemaphoreType.DMA((K,)),
        ],
        compiler_params=limit(BIG),
    )(pos, root, interim, up)


def run_up(mask_own, mask_part, own, part):
    block = pl.BlockSpec((1, 128, 2048), lambda k: (k, 0, 0))
    return pl.pallas_call(
        up_kernel,
        out_shape=pltpu.HBM((K, 512, 2048), BF16),
        grid=(K,),
        in_specs=[SMEM, SMEM, block, block],
        out_specs=pl.BlockSpec((1, 512, 2048), lambda k: (k, 0, 0)),
        compiler_params=limit(BIG),
    )(mask_own, mask_part, own, part)


def body(rhs_sub, rhs_root, lower_inv, upper_inv, coupling_low, coupling_up, tile_mask, root_inv):
    me = lax.axis_index("row")
    layer = lax.axis_index("layer")
    core = me % 2
    pos = jnp.stack([me // 8, me // 2 % 4, core]).astype(jnp.int32)
    first = core == 0

    def to_columns(a):
        left, right = a[..., :128], a[..., 128:]
        mine, other = jnp.where(first, left, right), jnp.where(first, right, left)
        got = swap(other)
        return jnp.where(
            first, jnp.concatenate([mine, got], axis=-2), jnp.concatenate([got, mine], axis=-2)
        )

    block = to_columns(rhs_sub[0])
    block, rhs_root, lower_own, low_own, up_own, root_inv, tile_mask = lax.optimization_barrier(
        (block, rhs_root, lower_inv[0], coupling_low[0], coupling_up[0], root_inv, tile_mask)
    )
    first_part, second_part, late = gather_plane(block)
    lower_part = swap(lower_own)
    mask_own = tile_mask[0]
    mask_part = swap(mask_own)
    right = lax.dynamic_slice_in_dim(to_columns(rhs_root).T, layer * 32, 32, 0)
    low_part = swap(low_own)
    up_part = swap(up_own)
    up = run_up(mask_own, mask_part, up_own, up_part)

    total = run_add(pos, FIRST, None, first_part, lower_own, lower_part)
    total = run_add(pos, SECOND, total, second_part, lower_own, lower_part)
    upper_own, root_inv = lax.optimization_barrier((upper_inv[0], root_inv, first_part[1]))[:2]
    upper_part = swap(upper_own)
    root_other = swap(root_inv)
    root_rows = jnp.where(
        first,
        jnp.concatenate([root_inv, root_other], axis=0),
        jnp.concatenate([root_other, root_inv], axis=0),
    )
    interim, parts = run_lower(
        pos, mask_own, mask_part, total, late, lower_own, lower_part, low_own, low_part
    )
    moved = lax.all_to_all(
        parts.reshape(64, 32, 128), ("layer", "row"), 0, 0, tiled=True,
        axis_index_groups=SAME_CORE_ALL,
    )
    reduced = right - jnp.sum(moved, axis=0)
    everywhere = lax.all_to_all(
        jnp.broadcast_to(reduced[None], (CH, 32, 128)), "row", 0, 0, tiled=True,
        axis_index_groups=SAME_CORE,
    )
    solved = jnp.einsum(
        "icr,oir->co", everywhere, root_rows.reshape(128, CH, 128), precision=lax.Precision.HIGHEST
    )
    root = lax.all_to_all(
        jnp.broadcast_to(solved[None], (64, 32, 128)), ("layer", "row"), 0, 0, tiled=True,
        axis_index_groups=SAME_CORE_ALL,
    ).reshape(4, CH, 32, 128)
    residue = run_couple(pos, root, interim, up)
    first_part, second_part, late = gather_plane(residue)
    total = run_add(pos, FIRST, None, first_part, upper_own, upper_part)
    total = run_add(pos, SECOND, total, second_part, upper_own, upper_part)
    out, out_part = run_upper(pos, total, late, upper_own, upper_part)
    sol_sub = lax.dynamic_update_slice(out, swap(out_part), (0, 0, (1 - core) * 128))

    chip = me // 2
    mine = lax.dynamic_index_in_dim(root, chip, 1, keepdims=False).reshape(128, 128).T
    own_rows = lax.dynamic_slice_in_dim(mine, core * 64, 64, 0)
    other_rows = swap(lax.dynamic_slice_in_dim(mine, (1 - core) * 64, 64, 0))
    sol_root = jnp.where(
        first,
        jnp.concatenate([own_rows, other_rows], axis=-1),
        jnp.concatenate([other_rows, own_rows], axis=-1),
    )
    return sol_sub[None], sol_root


def solution(mesh):
    return jax.shard_map(
        body,
        mesh=mesh,
        in_specs=(
            P("layer", None, "row", None),
            P("row", None),
            P("layer", None, "row", None),
            P("layer", None, "row", None),
            P("layer", None, None, "row"),
            P("layer", None, "row", None),
            P("layer", None, None, "row"),
            P("row", None),
        ),
        out_specs=(P("layer", None, "row", None), P("row", None)),
        check_vma=False,
    )
```

```python
import functools

import jax
import jax.numpy as jnp
from jax import lax
from jax.experimental import pallas as pl
from jax.experimental.pallas import tpu as pltpu
from jax.sharding import PartitionSpec as P


K = 3
CH = 16
F32 = jnp.float32
BF16 = jnp.bfloat16


def row_id(y, x, c):
    return (y % 4) * 8 + (x % 4) * 2 + c % 2


def shift(array, da, db):
    pairs = []
    for y in range(4):
        for x in range(4):
            pairs.append((row_id(y, x, 0), row_id(y + db, x + da, 0)))
            pairs.append((row_id(y, x, 1), row_id(y + da, x + db, 1)))
    return lax.ppermute(array, "row", pairs)


def swap(array):
    return lax.ppermute(array, "row", [(i, i ^ 1) for i in range(32)])


SAME_CORE = [[2 * i + c for i in range(CH)] for c in range(2)]
SAME_CORE_ALL = [[l * 32 + 2 * i + c for l in range(4) for i in range(CH)] for c in range(2)]

FIRST = [(0, 0), (1, 0), (-1, 0), (2, 0)]
SECOND = [(0, -1), (0, 1), (1, -1), (1, 1), (-1, -1), (-1, 1), (2, -1), (2, 1)]
LATE = [(0, 2), (1, 2), (-1, 2), (2, 2)]


def gather_plane(own):
    move = lambda v, da, db: shift(v, da, db)
    right, left = move(own, -1, 0), move(own, 1, 0)
    far = move(own, 2, 0)
    ups, downs = [], []
    for value in (own, right, left, far):
        ups.append(move(value, 0, 1))
        downs.append(move(value, 0, -1))
    late = [move(downs[0], 0, -1), move(downs[1], 0, -1), move(ups[2], 0, 1), move(downs[3], 0, -1)]
    second = [piece for pair in zip(ups, downs) for piece in pair]
    return [own, right, left, far], second, late


def halves(value):
    top = value.astype(BF16)
    return top, (value - top.astype(F32)).astype(BF16)


def stacked(value, axis):
    return jnp.concatenate(halves(value), axis=axis)


def product(rows, w):
    n = rows.shape[0] // 2
    wide = jnp.dot(rows, w, preferred_element_type=F32)
    tall = wide[:n] + wide[n:]
    return tall[:, :128] + tall[:, 128:]


def chip_of(pos, da, db):
    core = pos[2]
    dy, dx = db + core * (da - db), da + core * (db - da)
    return lax.rem(pos[0] + dy + 4, 4) * 4 + lax.rem(pos[1] + dx + 4, 4)


def start_stage(pos, stage, pieces, own, part, lv, pv, sems):
    columns = [
        pl.ds(pl.multiple_of(chip_of(pos, da, db) * 256, 256), 256) for da, db in stage
    ]
    waits = []
    for k in range(K):
        copies = []
        for j, piece in enumerate(pieces):
            copies.append((piece.at[k], pv.at[k, j]))
        for j, column in enumerate(columns):
            here = slice(j * 256, j * 256 + 256)
            copies.append((own.at[k, :, column], lv.at[k, 0:128, here]))
            copies.append((part.at[k, :, column], lv.at[k, 128:256, here]))
        copies = [
            pltpu.make_async_copy(src, dst, sems.at[k, i]) for i, (src, dst) in enumerate(copies)
        ]
        for copy in copies:
            copy.start()
        waits.append(copies)
    return waits


def stage_product(waits, k, lv, pv, w):
    for copy in waits[k]:
        copy.wait()
    for j in range(pv.shape[1]):
        w[k, j * 256 : j * 256 + 256, :] = stacked(pv[k, j], 1)
    return product(stacked(lv[k], 0), w[k])


def add_kernel(stage, has_total, pos, *refs):
    total, refs = (refs[0], refs[1:]) if has_total else (None, refs)
    pieces = refs[: len(stage)]
    own, part, out, lv, pv, w, sems = refs[len(stage) :]
    waits = start_stage(pos, stage, pieces, own, part, lv, pv, sems)
    for k in range(K):
        value = stage_product(waits, k, lv, pv, w)
        out[k] = total[k] + value if has_total else value


def lower_kernel(n, pos, mask_own, mask_part, total, *refs):
    pieces = refs[:n]
    own, part, low_own, low_part, interim, out, lv, pv, w, lo_v, lp_v, sems, low_sems = refs[n:]
    waits = start_stage(pos, LATE, pieces, own, part, lv, pv, sems)
    low_copies = []
    for c in range(4):
        rows = slice(c * 512, c * 512 + 512)
        low_copies.append(
            [
                pltpu.make_async_copy(low_own.at[:, rows], lo_v.at[:, rows], low_sems.at[c, 0]),
                pltpu.make_async_copy(low_part.at[:, rows], lp_v.at[:, rows], low_sems.at[c, 1]),
            ]
        )
        for copy in low_copies[-1]:
            copy.start()
    weights = []
    for k in range(K):
        value = total[k] + stage_product(waits, k, lv, pv, w)
        interim[k] = value
        weights.append(stacked(value, 1))
    for c in range(4):
        for copy in low_copies[c]:
            copy.wait()
        roots = None
        for k in range(K):
            tiles = []
            for i in range(4 * c, 4 * c + 4):
                rows = slice(i * 128, i * 128 + 128)
                tiles.append(
                    jnp.concatenate(
                        [
                            lo_v[k, rows, :] * mask_own[k, i, 0].astype(F32),
                            lp_v[k, rows, :] * mask_part[k, i, 0].astype(F32),
                        ],
                        axis=1,
                    )
                )
            value = product(stacked(jnp.concatenate(tiles, axis=0), 0), weights[k])
            roots = value if roots is None else roots + value
        for i in range(4):
            flat = roots[i * 128 : i * 128 + 128].T
            for z in range(4):
                out[z, 4 * c + i] = flat[z * 32 : z * 32 + 32]


def upper_kernel(n, pos, total, *refs):
    pieces = refs[:n]
    own, part, out, out_part, lv, pv, w, sems = refs[n:]
    waits = start_stage(pos, LATE, pieces, own, part, lv, pv, sems)
    lanes = pl.ds(pl.multiple_of(pos[2] * 128, 128), 128)
    for k in range(K):
        value = total[k] + stage_product(waits, k, lv, pv, w)
        out[k, :, lanes] = value[:128]
        out_part[k] = value[128:]


def couple_kernel(pos, root, interim, up, residue, w):
    for i in range(CH):
        flat = jnp.concatenate([root[z, i] for z in range(4)], axis=0)
        w[i * 128 : i * 128 + 128, :] = stacked(flat.T, 1)
    here = pl.ds(pl.multiple_of(pos[2] * 128, 128), 128)
    there = pl.ds(pl.multiple_of((1 - pos[2]) * 128, 128), 128)
    for k in range(K):
        value = interim[k] - product(up[k], w[...])
        residue[k, here, :] = value[:128]
        residue[k, there, :] = value[128:]


def up_kernel(mask_own, mask_part, own, part, out):
    k = pl.program_id(0)
    for n, (mask, ref) in enumerate(((mask_own, own), (mask_part, part))):
        for i in range(CH):
            lanes = slice(i * 128, i * 128 + 128)
            top, low = halves(ref[0, :, lanes] * mask[k, i, 0].astype(F32))
            out[0, n * 128 : n * 128 + 128, lanes] = top
            out[0, 256 + n * 128 : 384 + n * 128, lanes] = low


BIG = 63.5
VMEM = pl.BlockSpec(memory_space=pltpu.VMEM)
HBM = pl.BlockSpec(memory_space=pltpu.HBM)
SMEM = pl.BlockSpec(memory_space=pltpu.SMEM)


def sds(*shape, dtype=F32):
    return jax.ShapeDtypeStruct(shape, dtype)


def limit(mib):
    return pltpu.CompilerParams(vmem_limit_bytes=int(mib * 1024 * 1024))


def stage_scratch(stage, pieces):
    n = len(stage)
    return [
        pltpu.VMEM((K, 256, n * 256), F32),
        pltpu.VMEM((K, n, 256, 128), F32),
        pltpu.VMEM((K, n * 256, 256), BF16),
        pltpu.SemaphoreType.DMA((K, 2 * n + len(pieces))),
    ]


def run_add(pos, stage, total, pieces, own, part):
    totals = [] if total is None else [total]
    return pl.pallas_call(
        functools.partial(add_kernel, stage, total is not None),
        out_shape=sds(K, 256, 128),
        in_specs=[SMEM] + [VMEM] * len(totals) + [HBM] * (len(pieces) + 2),
        out_specs=VMEM,
        scratch_shapes=stage_scratch(stage, pieces),
        compiler_params=limit(BIG),
    )(pos, *totals, *pieces, own, part)


def run_lower(pos, mask_own, mask_part, total, pieces, own, part, low_own, low_part):
    scratch = stage_scratch(LATE, pieces)
    return pl.pallas_call(
        functools.partial(lower_kernel, len(pieces)),
        out_shape=(sds(K, 256, 128), sds(4, CH, 32, 128)),
        in_specs=[SMEM] * 3 + [VMEM] + [HBM] * (len(pieces) + 4),
        out_specs=(VMEM, VMEM),
        scratch_shapes=scratch[:3]
        + [
            pltpu.VMEM((K, 2048, 128), F32),
            pltpu.VMEM((K, 2048, 128), F32),
            scratch[3],
            pltpu.SemaphoreType.DMA((4, 2)),
        ],
        compiler_params=limit(BIG),
    )(pos, mask_own, mask_part, total, *pieces, own, part, low_own, low_part)


def run_upper(pos, total, pieces, own, part):
    return pl.pallas_call(
        functools.partial(upper_kernel, len(pieces)),
        out_shape=(sds(K, 128, 256), sds(K, 128, 128)),
        in_specs=[SMEM, VMEM] + [HBM] * (len(pieces) + 2),
        out_specs=(VMEM, VMEM),
        scratch_shapes=stage_scratch(LATE, pieces),
        compiler_params=limit(BIG),
    )(pos, total, *pieces, own, part)


def run_couple(pos, root, interim, up):
    return pl.pallas_call(
        couple_kernel,
        out_shape=sds(K, 256, 128),
        in_specs=[SMEM, VMEM, VMEM, VMEM],
        out_specs=VMEM,
        scratch_shapes=[pltpu.VMEM((2048, 256), BF16)],
        compiler_params=limit(36),
    )(pos, root, interim, up)


def run_up(mask_own, mask_part, own, part):
    block = pl.BlockSpec((1, 128, 2048), lambda k: (k, 0, 0))
    return pl.pallas_call(
        up_kernel,
        out_shape=pltpu.VMEM((K, 512, 2048), BF16),
        grid=(K,),
        in_specs=[SMEM, SMEM, block, block],
        out_specs=pl.BlockSpec((1, 512, 2048), lambda k: (k, 0, 0)),
        compiler_params=limit(36),
    )(mask_own, mask_part, own, part)


def body(rhs_sub, rhs_root, lower_inv, upper_inv, coupling_low, coupling_up, tile_mask, root_inv):
    me = lax.axis_index("row")
    layer = lax.axis_index("layer")
    core = me % 2
    pos = jnp.stack([me // 8, me // 2 % 4, core]).astype(jnp.int32)
    first = core == 0

    def to_columns(a):
        left, right = a[..., :128], a[..., 128:]
        mine, other = jnp.where(first, left, right), jnp.where(first, right, left)
        got = swap(other)
        return jnp.where(
            first, jnp.concatenate([mine, got], axis=-2), jnp.concatenate([got, mine], axis=-2)
        )

    block = to_columns(rhs_sub[0])
    block, rhs_root, lower_own, low_own, up_own, root_inv, tile_mask = lax.optimization_barrier(
        (block, rhs_root, lower_inv[0], coupling_low[0], coupling_up[0], root_inv, tile_mask)
    )
    first_part, second_part, late = gather_plane(block)
    lower_part = swap(lower_own)
    mask_own = tile_mask[0]
    mask_part = swap(mask_own)
    right = lax.dynamic_slice_in_dim(to_columns(rhs_root).T, layer * 32, 32, 0)
    low_part = swap(low_own)
    up_part = swap(up_own)
    up = run_up(mask_own, mask_part, up_own, up_part)

    total = run_add(pos, FIRST, None, first_part, lower_own, lower_part)
    total = run_add(pos, SECOND, total, second_part, lower_own, lower_part)
    upper_own, root_inv = lax.optimization_barrier((upper_inv[0], root_inv, first_part[1]))[:2]
    upper_part = swap(upper_own)
    root_other = swap(root_inv)
    root_rows = jnp.where(
        first,
        jnp.concatenate([root_inv, root_other], axis=0),
        jnp.concatenate([root_other, root_inv], axis=0),
    )
    interim, parts = run_lower(
        pos, mask_own, mask_part, total, late, lower_own, lower_part, low_own, low_part
    )
    moved = lax.all_to_all(
        parts.reshape(64, 32, 128), ("layer", "row"), 0, 0, tiled=True,
        axis_index_groups=SAME_CORE_ALL,
    )
    reduced = right - jnp.sum(moved, axis=0)
    everywhere = lax.all_to_all(
        jnp.broadcast_to(reduced[None], (CH, 32, 128)), "row", 0, 0, tiled=True,
        axis_index_groups=SAME_CORE,
    )
    solved = jnp.einsum(
        "icr,oir->co", everywhere, root_rows.reshape(128, CH, 128), precision=lax.Precision.HIGHEST
    )
    root = lax.all_to_all(
        jnp.broadcast_to(solved[None], (64, 32, 128)), ("layer", "row"), 0, 0, tiled=True,
        axis_index_groups=SAME_CORE_ALL,
    ).reshape(4, CH, 32, 128)
    residue = run_couple(pos, root, interim, up)
    first_part, second_part, late = gather_plane(residue)
    total = run_add(pos, FIRST, None, first_part, upper_own, upper_part)
    total = run_add(pos, SECOND, total, second_part, upper_own, upper_part)
    out, out_part = run_upper(pos, total, late, upper_own, upper_part)
    sol_sub = lax.dynamic_update_slice(out, swap(out_part), (0, 0, (1 - core) * 128))

    chip = me // 2
    mine = lax.dynamic_index_in_dim(root, chip, 1, keepdims=False).reshape(128, 128).T
    own_rows = lax.dynamic_slice_in_dim(mine, core * 64, 64, 0)
    other_rows = swap(lax.dynamic_slice_in_dim(mine, (1 - core) * 64, 64, 0))
    sol_root = jnp.where(
        first,
        jnp.concatenate([own_rows, other_rows], axis=-1),
        jnp.concatenate([other_rows, own_rows], axis=-1),
    )
    return sol_sub[None], sol_root


def solution(mesh):
    return jax.shard_map(
        body,
        mesh=mesh,
        in_specs=(
            P("layer", None, "row", None),
            P("row", None),
            P("layer", None, "row", None),
            P("layer", None, "row", None),
            P("layer", None, None, "row"),
            P("layer", None, "row", None),
            P("layer", None, None, "row"),
            P("row", None),
        ),
        out_specs=(P("layer", None, "row", None), P("row", None)),
        check_vma=False,
    )
```
